32 devices in a mesh: blk: 8 (over z, y), wide: 4 (over x, core).
Axes of the slice: x: 2, y: 2, z: 4, core: 2. Of those that a mesh axis runs over, the one named last changes fastest.
Arguments:
- query_rows: bfloat16 [4, 1024, 1536], P('wide', 'blk'), may hold values from -40 to 40
- key_rows: bfloat16 [4, 1024, 1536], P('wide', 'blk'), may hold values from -6 to 6
- value_rows: bfloat16 [4, 1024, 1536], P('wide', 'blk'), may hold values from -6 to 6
- patch_index: int32 [4, 1024], P('wide', 'blk'), may hold values from 0 to 4095, as said below
- live_count: int32 [4, 8], P('wide', 'blk'), may hold values from 64 to 128, as said below
- slopes: float32 [12], replicated, may hold values from 0.003 to 0.15
- out_weight: bfloat16 [1536, 1536], P('wide'), may hold values from -0.15625 to 0.15625
- out_grad: bfloat16 [4, 1024, 1536], P('wide', 'blk'), may hold values from -6 to 6
Outputs:
- layer_out: bfloat16 [4, 1024, 1536], P('wide', 'blk')
- grad_query: bfloat16 [4, 1024, 1536], P('wide', 'blk')
- grad_key: bfloat16 [4, 1024, 1536], P('wide', 'blk')
- grad_value: bfloat16 [4, 1024, 1536], P('wide', 'blk')
- grad_weight: float32 [1536, 1536], P('wide')
The draws below stay inside these ranges and needn't reach their ends.
Inputs may be any that keep to these rules, and one draw needn't show every extreme that they name: `patch_index`: within a slab b, the slots hold distinct patch numbers of the range b * 512 to (b + 1) * 512 - 1 in increasing order; slots beyond the live count hold such numbers too. `live_count`: every crop has a slab with exactly 128 live slots; the live slots of a slab are its first ones.
All inputs are finite; a program needn't handle non-finite values.
Results may differ from the reference program's by a relative error of at most 0.015.
Values may be sent and summed in bfloat16 or wider, within the bound.
A program may use at most 128 MiB of HBM per device.

```python
import math
import jax
import jax.numpy as jnp
from jax import lax

HEADS = 12
HEAD_DIM = 128
OUT_WIDTH = 1536
SIDE = 32
PATCH_DEV = 512
CAP = 128
INNER = 1536
VIS = 1024
CROPS = 4


def key_grid(key):
    seed_key = jax.random.fold_in(key, 11)
    slab_count = VIS // CAP
    grid = jnp.clip(jax.random.normal(seed_key, (CROPS, slab_count, CAP, INNER), jnp.float32), -6.0, 6.0)
    return grid


def draw_key_rows(key, part):
    grid = key_grid(key)
    return grid.reshape(CROPS, VIS, INNER).astype(jnp.bfloat16)


def draw_query_rows(key, part):
    slab_count = VIS // CAP
    seed_key = jax.random.fold_in(key, 23)
    grid = jnp.clip(jax.random.normal(seed_key, (CROPS, slab_count, CAP, INNER), jnp.float32), -6.0, 6.0)
    return grid.reshape(CROPS, VIS, INNER).astype(jnp.bfloat16)


def draw_patch_index(key, part):
    slab_count = VIS // CAP
    streams = jax.random.split(jax.random.fold_in(key, 31), CROPS * slab_count)
    chosen = jax.vmap(lambda stream: jax.random.permutation(stream, PATCH_DEV)[:CAP])(streams)
    chosen = jnp.sort(chosen.astype(jnp.int32), axis=1).reshape(CROPS, slab_count, CAP)
    offset = (jnp.arange(slab_count, dtype=jnp.int32) * PATCH_DEV)[None, :, None]
    return (chosen + offset).reshape(CROPS, VIS).astype(jnp.int32)


def draw_live_count(key, part):
    slab_count = VIS // CAP
    counts = jax.random.randint(jax.random.fold_in(key, 5), (CROPS, slab_count), CAP // 2, CAP + 1)
    fullest = jax.random.randint(jax.random.fold_in(key, 7), (CROPS, 1), 0, slab_count)
    return jnp.where(jnp.arange(slab_count)[None, :] == fullest, CAP, counts).astype(jnp.int32)


def shard_levels(stream_key, shape, shards, low, largest):
    gain = 1.0
    for dim, blocks in shards:
        steps = jax.random.uniform(jax.random.fold_in(jax.random.fold_in(stream_key, 6), dim), (blocks,), jnp.float32, low / len(shards), largest / len(shards))
        gain = gain * jnp.repeat(jnp.exp(steps), shape[dim] // blocks).reshape((-1,) + (1,) * (len(shape) - 1 - dim))
    return gain


def normal_values(key, dims, scale, most, shards=(), kind=jnp.bfloat16):
    loudness = shard_levels(key, dims, shards, -0.22, 0.18) if shards else 1.0
    entries = jax.random.normal(key, dims, jnp.float32) * scale * loudness
    return jnp.minimum(jnp.maximum(entries, -most), most).astype(kind)


def setup_inputs(seed: int = 0) -> dict:
    key_list = jax.random.split(jax.random.key(seed), 9)
    query_rows = draw_query_rows(jax.random.fold_in(key_list[8], 71), 0)
    key_rows = draw_key_rows(jax.random.fold_in(key_list[8], 71), 0)
    value_rows = normal_values(key_list[2], (CROPS, VIS, INNER), 1.0, 6.0, ((0, 4), (1, 8)))
    patch_index = draw_patch_index(jax.random.fold_in(key_list[8], 71), 0)
    live_count = draw_live_count(jax.random.fold_in(key_list[8], 71), 0)
    slopes = jnp.clip(jnp.exp(jax.random.uniform(key_list[5], (HEADS,), jnp.float32, math.log(0.003), math.log(0.15))), 0.003, 0.15)
    out_weight = normal_values(key_list[6], (INNER, OUT_WIDTH), INNER ** -0.5, 0.15625, ((0, 4),))
    out_grad = normal_values(key_list[7], (CROPS, VIS, OUT_WIDTH), 1.0, 6.0, ((0, 4), (1, 8)))
    return {"query_rows": query_rows, "key_rows": key_rows, "value_rows": value_rows, "patch_index": patch_index, "live_count": live_count, "slopes": slopes, "out_weight": out_weight, "out_grad": out_grad}


MASKED = -1.0e30


def coordinates(index):
    return index % SIDE, (index // SIDE) % SIDE, index // (SIDE * SIDE)


def spacing(row_index, col_index):
    row_x, row_y, row_z = coordinates(row_index)
    col_x, col_y, col_z = coordinates(col_index)
    distance = jnp.abs(row_x[:, None] - col_x[None, :]) + jnp.abs(row_y[:, None] - col_y[None, :]) + jnp.abs(row_z[:, None] - col_z[None, :])
    return distance.astype(jnp.float32)


def softmax_rows(query_part, key_part, row_index, col_index, key_live, slopes):
    scaling = HEAD_DIM ** -0.5
    query_heads = query_part.astype(jnp.float32).reshape(query_part.shape[0], HEADS, HEAD_DIM)
    key_heads = key_part.astype(jnp.float32).reshape(key_part.shape[0], HEADS, HEAD_DIM)
    scores = jnp.einsum("qhd,khd->hqk", query_heads, key_heads) * scaling
    scores = scores - slopes[:, None, None] * spacing(row_index, col_index)[None]
    scores = jnp.where(key_live[None, None, :], scores, MASKED)
    row_max = jnp.max(scores, axis=2, keepdims=True)
    row_lse = row_max + jnp.log(jnp.sum(jnp.exp(scores - row_max), axis=2, keepdims=True))
    return jnp.exp(scores - row_lse), row_lse[:, :, 0]


def rounded(value):
    return lax.optimization_barrier(value.astype(jnp.bfloat16)).astype(jnp.float32)


def one_crop(query_rows, key_rows, value_rows, patch_index, live_count, out_grad, out_weight, slopes):
    blocks = VIS // CAP
    scaling = HEAD_DIM ** -0.5
    position = jnp.arange(VIS, dtype=jnp.int32)
    live_slot = (position % CAP) < jnp.repeat(live_count, CAP)
    attn_prob, row_lse = softmax_rows(query_rows, key_rows, patch_index, patch_index, live_slot, slopes)
    prob_low = attn_prob.astype(jnp.bfloat16)
    value_heads = value_rows.astype(jnp.float32).reshape(VIS, HEADS, HEAD_DIM)
    key_heads = key_rows.astype(jnp.float32).reshape(VIS, HEADS, HEAD_DIM)
    attended = jnp.einsum("hqk,khd->qhd", prob_low.astype(jnp.float32), value_heads).reshape(VIS, INNER)
    attended = jnp.where(live_slot[:, None], attended, 0.0).astype(jnp.bfloat16)
    layer_out = jnp.dot(attended, out_weight, preferred_element_type=jnp.float32).astype(jnp.bfloat16)
    grad_att = jnp.dot(out_grad, out_weight.T, preferred_element_type=jnp.float32)
    grad_att = jnp.where(live_slot[:, None], grad_att, 0.0).astype(jnp.bfloat16)
    grad_heads = grad_att.astype(jnp.float32).reshape(VIS, HEADS, HEAD_DIM)
    grad_prob = jnp.einsum("qhd,khd->hqk", grad_heads, value_heads)
    row_delta = jnp.sum(attn_prob * grad_prob, axis=2, keepdims=True)
    grad_score = (attn_prob * (grad_prob - row_delta)).astype(jnp.bfloat16)
    grad_query = (jnp.einsum("hqk,khd->qhd", grad_score.astype(jnp.float32), key_heads) * scaling).reshape(VIS, INNER).astype(jnp.bfloat16)
    query_slabs = query_rows.astype(jnp.float32).reshape(blocks, CAP, HEADS, HEAD_DIM)
    score_slabs = grad_score.astype(jnp.float32).reshape(HEADS, blocks, CAP, VIS)
    prob_slabs = prob_low.astype(jnp.float32).reshape(HEADS, blocks, CAP, VIS)
    grad_slabs = grad_heads.reshape(blocks, CAP, HEADS, HEAD_DIM)
    key_terms = rounded(jnp.einsum("hbqk,bqhd->bkhd", score_slabs, query_slabs) * scaling)
    grad_key = jnp.sum(key_terms, axis=0).reshape(VIS, INNER).astype(jnp.bfloat16)
    value_terms = rounded(jnp.einsum("hbqk,bqhd->bkhd", prob_slabs, grad_slabs))
    grad_value = jnp.sum(value_terms, axis=0).reshape(VIS, INNER).astype(jnp.bfloat16)
    attended_slabs = attended.astype(jnp.float32).reshape(blocks, CAP, INNER)
    cotangent_slabs = out_grad.astype(jnp.float32).reshape(blocks, CAP, OUT_WIDTH)
    weight_terms = rounded(jnp.einsum("bqi,bqo->bio", attended_slabs, cotangent_slabs))
    return layer_out, grad_query, grad_key, grad_value, jnp.sum(weight_terms, axis=0)


def reference(query_rows, key_rows, value_rows, patch_index, live_count, slopes, out_weight, out_grad):
    def crop_step(carry, crop_items):
        query_part, key_part, value_part, index_part, count_part, grad_part = crop_items
        results = one_crop(query_part, key_part, value_part, index_part, count_part, grad_part, out_weight, slopes)
        return carry + results[4], results[:4]

    start_value = jnp.zeros((INNER, OUT_WIDTH), jnp.float32)
    grad_weight, stacked = lax.scan(crop_step, start_value, (query_rows, key_rows, value_rows, patch_index, live_count, out_grad))
    layer_out, grad_query, grad_key, grad_value = stacked
    return layer_out, grad_query, grad_key, grad_value, grad_weight
```

```python
import functools
import math

import jax
import jax.numpy as jnp
from jax import lax
from jax.experimental import pallas as pl
from jax.experimental.pallas import tpu as pltpu
from jax.sharding import PartitionSpec as P

HEADS = 12
HEAD_DIM = 128
SIDE = 32
FAR = 1e32
MESH = pl.DeviceIdType.MESH
BF = jnp.bfloat16
F32 = jnp.float32


def dot(a, b, ca, cb):
    return lax.dot_general(a, b, (((ca,), (cb,)), ((), ())), preferred_element_type=F32)


def kernel(
    n, m, G, slopes_ref, aux_ref, q_ref, k_ref, v_ref, w_ref, do_ref,
    lo_ref, dq_ref, dk_ref, dv_ref, gw_ref,
    aux_all, tpad, cols_all, pen, qg, kvg, gg, prob, attg, dqg, acc_k, acc_v,
    dkb, dkin, dkz, do_w, w_all, ga_out, ga_in, ga_full, att_full, att_parts, att_w, lo_acc,
    gwf, gwb, gs, gw_in, gz, gz_in, gout, send_sem, recv_sem,
):
    R = n // G
    H = HEADS // G
    D = HEAD_DIM
    S = q_ref.shape[0]
    wr = w_ref.shape[0]
    rows = wr // n
    scale = HEAD_DIM ** -0.5
    b = lax.axis_index("blk")
    w = lax.axis_index("wide")
    g = b // R
    r = b % R
    sent = []

    def put(src, dst, **device):
        i = len(sent)
        copy = pltpu.make_async_remote_copy(
            src_ref=src, dst_ref=dst, send_sem=send_sem.at[i], recv_sem=recv_sem.at[i],
            device_id=device, device_id_type=MESH,
        )
        copy.start()
        sent.append(copy)
        return copy

    def group(i):
        return (g + i) % G

    def lanes(group_index, h):
        return pl.ds(pl.multiple_of((group_index * H + h) * D, D), D)

    barrier = pltpu.get_barrier_semaphore()
    for i in range(1, n):
        pl.semaphore_signal(barrier, inc=1, device_id={"blk": (b + i) % n}, device_id_type=MESH)
    for i in range(1, m):
        pl.semaphore_signal(barrier, inc=1, device_id={"wide": (w + i) % m}, device_id_type=MESH)
    pl.semaphore_wait(barrier, n + m - 2)

    c_do = [put(do_ref, do_w.at[w], wide=(w + i) % m) for i in range(1, m)]
    c_aux = [put(aux_ref, aux_all.at[b], blk=(b + i) % n) for i in range(1, n)]
    c_kv, c_q = [], []
    for h in range(H):
        for i in range(1, G):
            there = group(i)
            peer = there * R + r
            c_kv.append((h, i, put(k_ref.at[:, lanes(there, h)], kvg.at[h, b, 0], blk=peer)))
            c_kv.append((h, i, put(v_ref.at[:, lanes(there, h)], kvg.at[h, b, 1], blk=peer)))
            c_q.append((h, put(q_ref.at[:, lanes(there, h)], qg.at[h, g], blk=peer)))

    c_fwd = {h: [] for h in range(H)}
    for h in range(H):
        kvg[h, b, 0] = k_ref[:, lanes(g, h)]
        kvg[h, b, 1] = v_ref[:, lanes(g, h)]
        qg[h, g] = q_ref[:, lanes(g, h)]
        for j in range(1, R):
            c_fwd[h].append(put(kvg.at[h, b], kvg.at[h, b], blk=g * R + (r + j) % R))
    do_w[w] = do_ref[...]
    w_all[w] = w_ref[...]
    aux_all[b] = aux_ref[...]

    for c in c_do:
        c.wait_recv()

    def ga_step(c, carry):
        ga_out[c] = dot(do_w[c], w_ref[...], 1, 1).astype(BF)
        return carry

    lax.fori_loop(0, m, ga_step, 0)
    c_ga = [put(ga_out.at[(w + i) % m], ga_in.at[w], wide=(w + i) % m) for i in range(1, m)]
    ga_in[w] = ga_out[w]
    c_w = [put(w_ref, w_all.at[w], wide=(w + i) % m) for i in range(1, m)]

    for c in c_aux:
        c.wait_recv()
    tpad[...] = jnp.zeros_like(tpad)

    def col_step(s, carry):
        tpad[0:8, :] = aux_all[s]
        cols_all[pl.ds(pl.multiple_of(s * S, S), S), :] = tpad[...].T
        return carry

    lax.fori_loop(0, n, col_step, 0)

    def pen_step(t, carry):
        row = aux_all[t * R + r]

        def one(s, inner):
            here = pl.ds(pl.multiple_of(s * S, S), S)
            col = cols_all[here, :]
            far = (
                jnp.abs(col[:, 0:1] - row[0:1, :])
                + jnp.abs(col[:, 1:2] - row[1:2, :])
                + jnp.abs(col[:, 2:3] - row[2:3, :])
            )
            pen[t, here, :] = jnp.where(col[:, 3:4] > 0.5, far, FAR)
            return inner

        lax.fori_loop(0, n, one, 0)
        return carry

    lax.fori_loop(0, G, pen_step, 0)

    def live_rows(t):
        start = pl.multiple_of((t * R + r) * S, S)
        return cols_all[pl.ds(start, S), :][:, 3:4] > 0.5

    def forward_kv(h):
        for hh, i, c in c_kv:
            if hh == h:
                c.wait_recv()
        for i in range(1, G):
            slab = ((g + G - i) % G) * R + r
            for j in range(1, R):
                c_fwd[h].append(put(kvg.at[h, slab], kvg.at[h, slab], blk=g * R + (r + j) % R))

    def fwd(h):
        for c in c_fwd[h]:
            c.wait_recv()
        for hh, c in c_q:
            if hh == h:
                c.wait_recv()
        slope = slopes_ref[g * H + h]

        def step(t, carry):
            s = dot(kvg[h, :, 0].reshape(n * S, D), qg[h, t], 1, 1) * scale - slope * pen[t]
            p = jnp.exp(s - jnp.max(s, axis=0, keepdims=True))
            p = p * (1.0 / jnp.sum(p, axis=0, keepdims=True))
            prob[h, t] = p
            att = dot(p.astype(BF), kvg[h, :, 1].reshape(n * S, D), 0, 0)
            attg[h, t] = jnp.where(live_rows(t), att, 0.0).astype(BF)
            return carry

        lax.fori_loop(0, G, step, 0)
        att_full[:, lanes(g, h)] = attg[h, g]
        return [
            put(attg.at[h, group(i)], att_full.at[:, lanes(g, h)], blk=group(i) * R + r)
            for i in range(1, G)
        ]

    forward_kv(0)

    for c in c_ga:
        c.wait_recv()
    for i in range(m):
        ga_full[:, i * wr : (i + 1) * wr] = ga_in[i]
    c_gg = {h: [] for h in range(H)}
    for h in range(H):
        gg[h, g] = ga_full[:, lanes(g, h)]
        for i in range(1, G):
            c_gg[h].append(
                put(ga_full.at[:, lanes(group(i), h)], gg.at[h, g], blk=group(i) * R + r)
            )

    c_att = []
    for h in range(H):
        if h + 1 < H:
            forward_kv(h + 1)
        c_att += fwd(h)

    c_dq, c_dk, c_dz = [], {}, []

    def bwd(h):
        for c in c_gg[h]:
            c.wait_recv()
        acc_k[h] = jnp.zeros((n * S, D), F32)
        acc_v[h] = jnp.zeros((n * S, D), F32)

        def step(t, carry):
            ga = gg[h, t]
            ga = jnp.where(live_rows(t), ga.astype(F32), 0.0).astype(BF)
            p = prob[h, t]
            gp = dot(kvg[h, :, 1].reshape(n * S, D), ga, 1, 1)
            delta = jnp.sum(p * gp, axis=0, keepdims=True)
            gs = (p * (gp - delta)).astype(BF)
            dqg[h, t] = (dot(gs, kvg[h, :, 0].reshape(n * S, D), 0, 0) * scale).astype(BF)
            acc_k[h] += dot(gs, qg[h, t], 1, 0) * scale
            acc_v[h] += dot(p.astype(BF), ga, 1, 0)
            return carry

        lax.fori_loop(0, G, step, 0)
        for rr in range(R):
            for t in range(G):
                at = (t * R + rr) * S
                dkb[h, rr, 0, t] = acc_k[h, at : at + S, :].astype(BF)
                dkb[h, rr, 1, t] = acc_v[h, at : at + S, :].astype(BF)
        c_dk[h] = [
            put(dkb.at[h, (r + j) % R], dkin.at[h, r], blk=g * R + (r + j) % R)
            for j in range(1, R)
        ]
        dq_ref[:, lanes(g, h)] = dqg[h, g]
        for i in range(1, G):
            c_dq.append(
                put(dqg.at[h, group(i)], dq_ref.at[:, lanes(g, h)], blk=group(i) * R + r)
            )

    def finish_keys(h):
        for c in c_dk[h]:
            c.wait_recv()

        def step(t, carry):
            here = pl.ds(pl.multiple_of((t * R + r) * S, S), S)
            total_k = acc_k[h, here, :]
            total_v = acc_v[h, here, :]
            for j in range(1, R):
                total_k += dkin[h, (r + j) % R, 0, t].astype(F32)
                total_v += dkin[h, (r + j) % R, 1, t].astype(F32)
            dkz[h, 0, t] = total_k.astype(BF)
            dkz[h, 1, t] = total_v.astype(BF)
            return carry

        lax.fori_loop(0, G, step, 0)
        dk_ref[:, lanes(g, h)] = dkz[h, 0, g]
        dv_ref[:, lanes(g, h)] = dkz[h, 1, g]
        for i in range(1, G):
            peer = group(i) * R + r
            c_dz.append(put(dkz.at[h, 0, group(i)], dk_ref.at[:, lanes(g, h)], blk=peer))
            c_dz.append(put(dkz.at[h, 1, group(i)], dv_ref.at[:, lanes(g, h)], blk=peer))

    bwd(0)

    for c in c_att:
        c.wait_recv()
    for i in range(m):
        att_parts[i] = att_full[:, i * wr : (i + 1) * wr]
    c_aw = [put(att_parts.at[(w + i) % m], att_w.at[w], wide=(w + i) % m) for i in range(1, m)]
    att_w[w] = att_parts[w]

    bwd(1)
    finish_keys(0)

    for c in c_aw:
        c.wait_recv()
    width = do_ref.shape[1]
    chunk = 512

    def gw_step(s, carry):
        here = pl.ds(pl.multiple_of(s * chunk, chunk), chunk)
        gwf[:, here] = dot(att_w[...].reshape(m * S, wr), do_w[:, :, here].reshape(m * S, chunk), 0, 0)
        return carry

    lax.fori_loop(0, width // chunk, gw_step, 0)
    for rr in range(R):
        for t in range(G):
            at = (rr * G + t) * rows
            gwb[rr, t] = gwf[at : at + rows, :]
    c_g1 = []
    for j in range(1, R):
        there = (r + j) % R
        gs[there] = gwb[there].astype(BF)
        c_g1.append(put(gs.at[there], gw_in.at[r], blk=g * R + there))

    for h in range(2, H):
        bwd(h)
        finish_keys(h - 1)

    for c in c_g1:
        c.wait_recv()

    def g1_step(t, carry):
        total = gwb[r, t]
        for j in range(1, R):
            total += gw_in[(r + j) % R, t].astype(F32)
        gz[t] = total.astype(BF)
        return carry

    lax.fori_loop(0, G, g1_step, 0)
    c_g2 = [put(gz.at[group(i)], gz_in.at[g], blk=group(i) * R + r) for i in range(1, G)]
    finish_keys(H - 1)

    for c in c_w:
        c.wait_recv()
    lo_acc[...] = jnp.zeros_like(lo_acc)

    def lo_step(i, carry):
        lo_acc[...] += dot(att_parts[i], w_all[i], 1, 0)
        return carry

    lax.fori_loop(0, m, lo_step, 0)
    lo_ref[...] = lo_acc[...].astype(BF)

    for c in c_g2:
        c.wait_recv()
    total = gz[g].astype(F32)
    for i in range(1, G):
        total += gz_in[group(i)].astype(F32)
    gout[r, g] = total.astype(BF)
    c_g3 = [put(gout.at[r, g], gout.at[r, g], blk=group(i) * R + r) for i in range(1, G)]
    for c in c_g3:
        c.wait_recv()
    c_g4 = [put(gout.at[r], gout.at[r], blk=g * R + (r + j) % R) for j in range(1, R)]
    for c in c_g4:
        c.wait_recv()
    for rr in range(R):
        for t in range(G):
            at = (rr * G + t) * rows
            gw_ref[at : at + rows, :] = gout[rr, t].astype(F32)
    for c in c_dq + c_dz:
        c.wait_recv()
    for c in sent:
        c.wait_send()


def body(query_rows, key_rows, value_rows, patch_index, live_count, slopes, out_weight, out_grad):
    n = lax.axis_size("blk")
    m = lax.axis_size("wide")
    G = math.gcd(HEADS, n)
    R = n // G
    H = HEADS // G
    S, inner = query_rows.shape[1:]
    wr, width = out_weight.shape
    rows = wr // n
    D = HEAD_DIM
    index = patch_index[0]
    live = jnp.arange(S, dtype=jnp.int32) < live_count[0, 0]
    zero = jnp.zeros((S,), jnp.int32)
    aux = jnp.stack(
        [index % SIDE, index // SIDE % SIDE, index // (SIDE * SIDE), live.astype(jnp.int32)] + [zero] * 4
    ).astype(F32)
    per = 2 * H * (G - 1) + H * (G - 1)
    copies = (
        3 * (m - 1) + (n - 1) + per + H * G * (R - 1) + H * (G - 1) * 5 + H * (R - 1)
        + (m - 1) + 2 * (R - 1) + 2 * (G - 1)
    )
    vmem = pl.BlockSpec(memory_space=pltpu.VMEM)
    outs = pl.pallas_call(
        functools.partial(kernel, n, m, G),
        out_shape=[jax.ShapeDtypeStruct((S, inner), BF)] * 4 + [jax.ShapeDtypeStruct((wr, width), F32)],
        in_specs=[pl.BlockSpec(memory_space=pltpu.SMEM)] + [vmem] * 6,
        out_specs=[vmem] * 5,
        scratch_shapes=[
            pltpu.VMEM((n, 8, S), F32),
            pltpu.VMEM((128, S), F32),
            pltpu.VMEM((n * S, 128), F32),
            pltpu.VMEM((G, n * S, S), F32),
            pltpu.VMEM((H, G, S, D), BF),
            pltpu.VMEM((H, n, 2, S, D), BF),
            pltpu.VMEM((H, G, S, D), BF),
            pltpu.VMEM((H, G, n * S, S), F32),
            pltpu.VMEM((H, G, S, D), BF),
            pltpu.VMEM((H, G, S, D), BF),
            pltpu.VMEM((H, n * S, D), F32),
            pltpu.VMEM((H, n * S, D), F32),
            pltpu.VMEM((H, R, 2, G, S, D), BF),
            pltpu.VMEM((H, R, 2, G, S, D), BF),
            pltpu.VMEM((H, 2, G, S, D), BF),
            pltpu.VMEM((m, S, width), BF),
            pltpu.VMEM((m, wr, width), BF),
            pltpu.VMEM((m, S, wr), BF),
            pltpu.VMEM((m, S, wr), BF),
            pltpu.VMEM((S, inner), BF),
            pltpu.VMEM((S, inner), BF),
            pltpu.VMEM((m, S, wr), BF),
            pltpu.VMEM((m, S, wr), BF),
            pltpu.VMEM((S, width), F32),
            pltpu.VMEM((wr, width), F32),
            pltpu.VMEM((R, G, rows, width), F32),
            pltpu.VMEM((R, G, rows, width), BF),
            pltpu.VMEM((R, G, rows, width), BF),
            pltpu.VMEM((G, rows, width), BF),
            pltpu.VMEM((G, rows, width), BF),
            pltpu.VMEM((R, G, rows, width), BF),
            pltpu.SemaphoreType.DMA((copies,)),
            pltpu.SemaphoreType.DMA((copies,)),
        ],
        compiler_params=pltpu.CompilerParams(
            collective_id=0, has_side_effects=True, vmem_limit_bytes=56 * 1024 * 1024
        ),
    )(slopes, aux, query_rows[0], key_rows[0], value_rows[0], out_weight, out_grad[0])
    return outs[0][None], outs[1][None], outs[2][None], outs[3][None], outs[4]


def solution(mesh):
    rows = P("wide", "blk", None)
    placed = (rows, rows, rows, P("wide", "blk"), P("wide", "blk"), P(), P("wide", None), rows)
    return jax.shard_map(
        body,
        mesh=mesh,
        in_specs=placed,
        out_specs=(rows, rows, rows, rows, P("wide", None)),
        check_vma=False,
    )
```

```python
import functools
import math

import jax
import jax.numpy as jnp
from jax import lax
from jax.experimental import pallas as pl
from jax.experimental.pallas import tpu as pltpu
from jax.sharding import PartitionSpec as P

HEADS = 12
HEAD_DIM = 128
SIDE = 32
FAR = 1e32
MESH = pl.DeviceIdType.MESH
BF = jnp.bfloat16
F32 = jnp.float32


def dot(a, b, ca, cb):
    return lax.dot_general(a, b, (((ca,), (cb,)), ((), ())), preferred_element_type=F32)


def kernel(
    n, m, G, slopes_ref, aux_ref, q_ref, k_ref, v_ref, w_ref, do_ref,
    lo_ref, dq_ref, dk_ref, dv_ref, gw_ref,
    aux_all, tpad, cols_all, pen, qg, kvg, gg, prob, attg, dqg, acc_k, acc_v,
    dkb, dkin, dkz, do_w, w_all, ga_out, ga_in, ga_full, att_full, att_parts, att_w, lo_acc,
    gwb, gs, gw_in, gz, gz_in, gout, send_sem, recv_sem,
):
    R = n // G
    H = HEADS // G
    D = HEAD_DIM
    S = q_ref.shape[0]
    wr = w_ref.shape[0]
    rows = wr // n
    scale = HEAD_DIM ** -0.5
    b = lax.axis_index("blk")
    w = lax.axis_index("wide")
    g = b // R
    r = b % R
    sent = []

    def put(src, dst, **device):
        i = len(sent)
        copy = pltpu.make_async_remote_copy(
            src_ref=src, dst_ref=dst, send_sem=send_sem.at[i], recv_sem=recv_sem.at[i],
            device_id=device, device_id_type=MESH,
        )
        copy.start()
        sent.append(copy)
        return copy

    def group(i):
        return (g + i) % G

    def lanes(group_index, h):
        return pl.ds(pl.multiple_of((group_index * H + h) * D, D), D)

    barrier = pltpu.get_barrier_semaphore()
    for i in range(1, n):
        pl.semaphore_signal(barrier, inc=1, device_id={"blk": (b + i) % n}, device_id_type=MESH)
    for i in range(1, m):
        pl.semaphore_signal(barrier, inc=1, device_id={"wide": (w + i) % m}, device_id_type=MESH)
    pl.semaphore_wait(barrier, n + m - 2)

    pairs = m // 2
    other = (w // 2) * 2 + (w + 1) % 2

    def away(i):
        return (w + 2 * i) % m

    c_do = [put(do_ref, do_w.at[w], wide=away(i)) for i in range(1, pairs)]
    c_do2 = [put(do_ref, do_w.at[w], wide=other)]
    c_aux = [put(aux_ref, aux_all.at[b], blk=(b + i) % n) for i in range(1, n)]
    c_kv, c_q = [], []
    for h in range(H):
        for i in range(1, G):
            there = group(i)
            peer = there * R + r
            c_kv.append((h, i, put(k_ref.at[:, lanes(there, h)], kvg.at[h, b, 0], blk=peer)))
            c_kv.append((h, i, put(v_ref.at[:, lanes(there, h)], kvg.at[h, b, 1], blk=peer)))
            c_q.append((h, put(q_ref.at[:, lanes(there, h)], qg.at[h, g], blk=peer)))

    c_fwd = {h: [] for h in range(H)}
    for h in range(H):
        kvg[h, b, 0] = k_ref[:, lanes(g, h)]
        kvg[h, b, 1] = v_ref[:, lanes(g, h)]
        qg[h, g] = q_ref[:, lanes(g, h)]
        for j in range(1, R):
            c_fwd[h].append(put(kvg.at[h, b], kvg.at[h, b], blk=g * R + (r + j) % R))
    do_w[w] = do_ref[...]
    w_all[w] = w_ref[...]
    aux_all[b] = aux_ref[...]

    for i, c in enumerate(c_do, 1):
        c.wait_recv()
        c_do2.append(put(do_w.at[away(pairs - i)], do_w.at[away(pairs - i)], wide=other))
    for c in c_do2:
        c.wait_recv()

    def ga_step(c, carry):
        ga_out[c] = dot(do_w[c], w_ref[...], 1, 1).astype(BF)
        return carry

    lax.fori_loop(0, m, ga_step, 0)
    c_ga = [put(ga_out.at[(w + i) % m], ga_in.at[w], wide=(w + i) % m) for i in range(1, m)]
    ga_in[w] = ga_out[w]
    c_w = [put(w_ref, w_all.at[w], wide=away(i)) for i in range(1, pairs)]
    c_w2 = [put(w_ref, w_all.at[w], wide=other)]

    for c in c_aux:
        c.wait_recv()
    tpad[...] = jnp.zeros_like(tpad)

    def col_step(s, carry):
        tpad[0:8, :] = aux_all[s]
        cols_all[pl.ds(pl.multiple_of(s * S, S), S), :] = tpad[...].T
        return carry

    lax.fori_loop(0, n, col_step, 0)

    def pen_step(t, carry):
        row = aux_all[t * R + r]

        def one(s, inner):
            here = pl.ds(pl.multiple_of(s * S, S), S)
            col = cols_all[here, :]
            far = (
                jnp.abs(col[:, 0:1] - row[0:1, :])
                + jnp.abs(col[:, 1:2] - row[1:2, :])
                + jnp.abs(col[:, 2:3] - row[2:3, :])
            )
            pen[t, here, :] = jnp.where(col[:, 3:4] > 0.5, far, FAR)
            return inner

        lax.fori_loop(0, n, one, 0)
        return carry

    lax.fori_loop(0, G, pen_step, 0)

    def live_rows(t):
        start = pl.multiple_of((t * R + r) * S, S)
        return cols_all[pl.ds(start, S), :][:, 3:4] > 0.5

    def forward_kv(h):
        for hh, i, c in c_kv:
            if hh == h:
                c.wait_recv()
        for i in range(1, G):
            slab = ((g + G - i) % G) * R + r
            for j in range(1, R):
                c_fwd[h].append(put(kvg.at[h, slab], kvg.at[h, slab], blk=g * R + (r + j) % R))

    def fwd(h):
        for c in c_fwd[h]:
            c.wait_recv()
        for hh, c in c_q:
            if hh == h:
                c.wait_recv()
        slope = slopes_ref[g * H + h]

        def step(t, carry):
            s = dot(kvg[h, :, 0].reshape(n * S, D), qg[h, t], 1, 1) * scale - slope * pen[t]
            p = jnp.exp(s - jnp.max(s, axis=0, keepdims=True))
            p = p * (1.0 / jnp.sum(p, axis=0, keepdims=True))
            prob[h, t] = p
            att = dot(p.astype(BF), kvg[h, :, 1].reshape(n * S, D), 0, 0)
            attg[h, t] = jnp.where(live_rows(t), att, 0.0).astype(BF)
            return carry

        lax.fori_loop(0, G, step, 0)
        att_full[:, lanes(g, h)] = attg[h, g]
        return [
            put(attg.at[h, group(i)], att_full.at[:, lanes(g, h)], blk=group(i) * R + r)
            for i in range(1, G)
        ]

    forward_kv(0)

    for c in c_ga:
        c.wait_recv()
    for i in range(m):
        ga_full[:, i * wr : (i + 1) * wr] = ga_in[i]
    c_gg = {h: [] for h in range(H)}
    for h in range(H):
        gg[h, g] = ga_full[:, lanes(g, h)]
        for i in range(1, G):
            c_gg[h].append(
                put(ga_full.at[:, lanes(group(i), h)], gg.at[h, g], blk=group(i) * R + r)
            )

    c_att = []
    for h in range(H):
        if h + 1 < H:
            forward_kv(h + 1)
        c_att += fwd(h)

    c_dq, c_dk, c_dz = [], {}, []

    def bwd(h):
        for c in c_gg[h]:
            c.wait_recv()
        acc_k[h] = jnp.zeros((n * S, D), F32)
        acc_v[h] = jnp.zeros((n * S, D), F32)

        def step(t, carry):
            ga = gg[h, t]
            ga = jnp.where(live_rows(t), ga.astype(F32), 0.0).astype(BF)
            p = prob[h, t]
            gp = dot(kvg[h, :, 1].reshape(n * S, D), ga, 1, 1)
            delta = jnp.sum(p * gp, axis=0, keepdims=True)
            gs = (p * (gp - delta)).astype(BF)
            dqg[h, t] = (dot(gs, kvg[h, :, 0].reshape(n * S, D), 0, 0) * scale).astype(BF)
            acc_k[h] += dot(gs, qg[h, t], 1, 0) * scale
            acc_v[h] += dot(p.astype(BF), ga, 1, 0)
            return carry

        lax.fori_loop(0, G, step, 0)
        for rr in range(R):
            for t in range(G):
                at = (t * R + rr) * S
                dkb[h, rr, 0, t] = acc_k[h, at : at + S, :].astype(BF)
                dkb[h, rr, 1, t] = acc_v[h, at : at + S, :].astype(BF)
        c_dk[h] = [
            put(dkb.at[h, (r + j) % R], dkin.at[h, r], blk=g * R + (r + j) % R)
            for j in range(1, R)
        ]
        dq_ref[:, lanes(g, h)] = dqg[h, g]
        for i in range(1, G):
            c_dq.append(
                put(dqg.at[h, group(i)], dq_ref.at[:, lanes(g, h)], blk=group(i) * R + r)
            )

    def finish_keys(h):
        for c in c_dk[h]:
            c.wait_recv()

        def step(t, carry):
            here = pl.ds(pl.multiple_of((t * R + r) * S, S), S)
            total_k = acc_k[h, here, :]
            total_v = acc_v[h, here, :]
            for j in range(1, R):
                total_k += dkin[h, (r + j) % R, 0, t].astype(F32)
                total_v += dkin[h, (r + j) % R, 1, t].astype(F32)
            dkz[h, 0, t] = total_k.astype(BF)
            dkz[h, 1, t] = total_v.astype(BF)
            return carry

        lax.fori_loop(0, G, step, 0)
        dk_ref[:, lanes(g, h)] = dkz[h, 0, g]
        dv_ref[:, lanes(g, h)] = dkz[h, 1, g]
        for i in range(1, G):
            peer = group(i) * R + r
            c_dz.append(put(dkz.at[h, 0, group(i)], dk_ref.at[:, lanes(g, h)], blk=peer))
            c_dz.append(put(dkz.at[h, 1, group(i)], dv_ref.at[:, lanes(g, h)], blk=peer))

    bwd(0)

    for c in c_att:
        c.wait_recv()
    for i in range(m):
        att_parts[i] = att_full[:, i * wr : (i + 1) * wr]
    c_aw = [put(att_parts.at[(w + i) % m], att_w.at[w], wide=(w + i) % m) for i in range(1, m)]
    att_w[w] = att_parts[w]

    bwd(1)

    for c in c_aw:
        c.wait_recv()
    chunk = gs.shape[-1]
    chunks = gs.shape[0]
    c_g1 = []
    for s in range(chunks):
        here = slice(s * chunk, (s + 1) * chunk)
        part = dot(att_w[...].reshape(m * S, wr), do_w[:, :, here].reshape(m * S, chunk), 0, 0)
        for rr in range(R):
            for t in range(G):
                at = (rr * G + t) * rows
                gwb[s, rr, t] = part[at : at + rows, :]
        c_g1.append([])
        for j in range(1, R):
            there = (r + j) % R
            gs[s, there] = gwb[s, there].astype(BF)
            c_g1[s].append(put(gs.at[s, there], gw_in.at[s, r], blk=g * R + there))

    finish_keys(0)
    for i, c in enumerate(c_w, 1):
        c.wait_recv()
        c_w2.append(put(w_all.at[away(pairs - i)], w_all.at[away(pairs - i)], wide=other))

    for h in range(2, H):
        bwd(h)
        finish_keys(h - 1)

    c_g2, c_g3, c_g4 = {}, {}, []

    def in_group(s):
        for c in c_g1[s]:
            c.wait_recv()
        total = gwb[s, r]
        for j in range(1, R):
            total += gw_in[s, (r + j) % R].astype(F32)
        gz[s] = total.astype(BF)
        c_g2[s] = [
            put(gz.at[s, group(i)], gz_in.at[s, g], blk=group(i) * R + r) for i in range(1, G)
        ]

    def over_groups(s):
        for c in c_g2[s]:
            c.wait_recv()
        total = gz[s, g].astype(F32)
        for i in range(1, G):
            total += gz_in[s, group(i)].astype(F32)
        gout[s, r, g] = total.astype(BF)
        c_g3[s] = [
            put(gout.at[s, r, g], gout.at[s, r, g], blk=group(i) * R + r) for i in range(1, G)
        ]

    def spread(s):
        for c in c_g3[s]:
            c.wait_recv()
        for j in range(1, R):
            c_g4.append(put(gout.at[s, r], gout.at[s, r], blk=g * R + (r + j) % R))

    for tick in range(chunks + 2):
        if tick < chunks:
            in_group(tick)
        if 1 <= tick <= chunks:
            over_groups(tick - 1)
        if tick == 1:
            finish_keys(H - 1)
        if tick >= 2:
            spread(tick - 2)

    for c in c_w2:
        c.wait_recv()
    lo_acc[...] = jnp.zeros_like(lo_acc)

    def lo_step(i, carry):
        lo_acc[...] += dot(att_parts[i], w_all[i], 1, 0)
        return carry

    lax.fori_loop(0, m, lo_step, 0)
    lo_ref[...] = lo_acc[...].astype(BF)

    for c in c_g4:
        c.wait_recv()
    for s in range(chunks):
        for rr in range(R):
            for t in range(G):
                at = (rr * G + t) * rows
                gw_ref[at : at + rows, s * chunk : (s + 1) * chunk] = gout[s, rr, t].astype(F32)
    for c in c_dq + c_dz:
        c.wait_recv()
    for c in sent:
        c.wait_send()


def body(query_rows, key_rows, value_rows, patch_index, live_count, slopes, out_weight, out_grad):
    n = lax.axis_size("blk")
    m = lax.axis_size("wide")
    G = math.gcd(HEADS, n)
    R = n // G
    H = HEADS // G
    S, inner = query_rows.shape[1:]
    wr, width = out_weight.shape
    rows = wr // n
    D = HEAD_DIM
    NC = width // 512
    index = patch_index[0]
    live = jnp.arange(S, dtype=jnp.int32) < live_count[0, 0]
    zero = jnp.zeros((S,), jnp.int32)
    aux = jnp.stack(
        [index % SIDE, index // SIDE % SIDE, index // (SIDE * SIDE), live.astype(jnp.int32)] + [zero] * 4
    ).astype(F32)
    per = 2 * H * (G - 1) + H * (G - 1)
    copies = (
        3 * (m - 1) + (n - 1) + per + H * G * (R - 1) + H * (G - 1) * 5 + H * (R - 1)
        + (m - 1) + NC * (2 * (R - 1) + 2 * (G - 1))
    )
    vmem = pl.BlockSpec(memory_space=pltpu.VMEM)
    outs = pl.pallas_call(
        functools.partial(kernel, n, m, G),
        out_shape=[jax.ShapeDtypeStruct((S, inner), BF)] * 4 + [jax.ShapeDtypeStruct((wr, width), F32)],
        in_specs=[pl.BlockSpec(memory_space=pltpu.SMEM)] + [vmem] * 6,
        out_specs=[vmem] * 5,
        scratch_shapes=[
            pltpu.VMEM((n, 8, S), F32),
            pltpu.VMEM((128, S), F32),
            pltpu.VMEM((n * S, 128), F32),
            pltpu.VMEM((G, n * S, S), F32),
            pltpu.VMEM((H, G, S, D), BF),
            pltpu.VMEM((H, n, 2, S, D), BF),
            pltpu.VMEM((H, G, S, D), BF),
            pltpu.VMEM((H, G, n * S, S), F32),
            pltpu.VMEM((H, G, S, D), BF),
            pltpu.VMEM((H, G, S, D), BF),
            pltpu.VMEM((H, n * S, D), F32),
            pltpu.VMEM((H, n * S, D), F32),
            pltpu.VMEM((H, R, 2, G, S, D), BF),
            pltpu.VMEM((H, R, 2, G, S, D), BF),
            pltpu.VMEM((H, 2, G, S, D), BF),
            pltpu.VMEM((m, S, width), BF),
            pltpu.VMEM((m, wr, width), BF),
            pltpu.VMEM((m, S, wr), BF),
            pltpu.VMEM((m, S, wr), BF),
            pltpu.VMEM((S, inner), BF),
            pltpu.VMEM((S, inner), BF),
            pltpu.VMEM((m, S, wr), BF),
            pltpu.VMEM((m, S, wr), BF),
            pltpu.VMEM((S, width), F32),
            pltpu.VMEM((NC, R, G, rows, width // NC), F32),
            pltpu.VMEM((NC, R, G, rows, width // NC), BF),
            pltpu.VMEM((NC, R, G, rows, width // NC), BF),
            pltpu.VMEM((NC, G, rows, width // NC), BF),
            pltpu.VMEM((NC, G, rows, width // NC), BF),
            pltpu.VMEM((NC, R, G, rows, width // NC), BF),
            pltpu.SemaphoreType.DMA((copies,)),
            pltpu.SemaphoreType.DMA((copies,)),
        ],
        compiler_params=pltpu.CompilerParams(
            collective_id=0, has_side_effects=True, vmem_limit_bytes=56 * 1024 * 1024
        ),
    )(slopes, aux, query_rows[0], key_rows[0], value_rows[0], out_weight, out_grad[0])
    return outs[0][None], outs[1][None], outs[2][None], outs[3][None], outs[4]


def solution(mesh):
    rows = P("wide", "blk", None)
    placed = (rows, rows, rows, P("wide", "blk"), P("wide", "blk"), P(), P("wide", None), rows)
    return jax.shard_map(
        body,
        mesh=mesh,
        in_specs=placed,
        out_specs=(rows, rows, rows, rows, P("wide", None)),
        check_vma=False,
    )
```
